32 devices in a mesh: walker: 2 (over core), slab: 2 (over x), chol: 8 (over z, y).
Axes of the slice: x: 2, y: 2, z: 4, core: 2. Of those that a mesh axis runs over, the one named last changes fastest.
Arguments:
- cholesky_factors: bfloat16 [96, 256, 2048], P('chol', None, 'slab'), may hold values from -0.13183594 to 0.13183594
- greens: bfloat16 [2, 256, 2048], P('walker', 'chol', 'slab'), may hold values from -1.7265625 to 1.7265625
- walker_weights: float32 [2], P('walker'), may hold values from 0.3 to 3
Outputs:
- fock: float32 [256, 2048], P(('walker', 'chol'), 'slab')
The draws below stay inside these ranges and needn't reach their ends.
All inputs are finite; a program needn't handle non-finite values.
Results may differ from the reference program's by a relative error of at most 0.0029.
Values may be sent and summed in bfloat16 or wider, within the bound.
A program may use at most 64 MiB of HBM per device.

```python
import math
import jax
import jax.numpy as jnp
from jax import lax

NORB = 2048
OCCUPIED_COUNT = 256
CHOLESKY_COUNT = 96
WALKERS = 2


def shard_levels(own_key, dims, split, smallest, largest):
    loudness = 1.0
    for axis_at, parts in split:
        steps = jax.random.uniform(jax.random.fold_in(jax.random.fold_in(own_key, 6), axis_at), (parts,), jnp.float32, smallest / len(split), largest / len(split))
        loudness = loudness * jnp.repeat(jnp.exp(steps), dims[axis_at] // parts).reshape((-1,) + (1,) * (len(dims) - 1 - axis_at))
    return loudness


def noise(key, extent, spread, most, cuts=(), kind=jnp.bfloat16):
    values = jax.random.normal(key, extent, jnp.float32) * spread
    if len(cuts) > 0:
        values = shard_levels(key, extent, cuts, -0.22, 0.18) * values
    return jnp.clip(values, min=-most, max=most).astype(kind)


def setup_inputs(seed: int = 0) -> dict:
    keys = jax.random.split(jax.random.key(seed), 4)
    cholesky_factors = noise(keys[0], (CHOLESKY_COUNT, OCCUPIED_COUNT, NORB), (NORB ** -0.5), 0.13183594, ((0, 8), (2, 2)))
    greens = noise(keys[1], (WALKERS, OCCUPIED_COUNT, NORB), ((NORB * 1.0) ** 0.5 * (OCCUPIED_COUNT * CHOLESKY_COUNT) ** -0.5), 1.7265625, ((0, 2), (1, 8), (2, 2)))
    walker_weights = jnp.clip(jnp.exp(math.log(3.0) - 2.3025851 * jax.random.uniform(keys[2], (WALKERS,), jnp.float32) ** shard_levels(keys[2], (WALKERS,), ((0, 2),), -0.2, 0.2)), 0.3, 3.0)
    return dict(cholesky_factors=cholesky_factors, greens=greens, walker_weights=walker_weights)


def reference(cholesky_factors, greens, walker_weights):
    factors_wide = cholesky_factors.astype(jnp.float32)

    def one_walker(inputs):
        theta, weight = inputs
        margin = jnp.einsum("gnp,mp->gnm", factors_wide, theta.astype(jnp.float32)).astype(jnp.bfloat16)
        terms = jnp.einsum("gnm,gmp->np", margin.astype(jnp.float32), factors_wide)
        return weight * terms

    per_walker = lax.map(one_walker, (greens, walker_weights))
    return jnp.sum(per_walker, axis=0)
```

```python
import functools

import jax
import jax.numpy as jnp
from jax import lax
from jax.experimental import pallas as pl
from jax.experimental.pallas import tpu as pltpu
from jax.sharding import PartitionSpec as P

MESH = pl.DeviceIdType.MESH
NT = (((1,), (1,)), ((), ()))
VMEM_LIMIT = 56000000


def exchange_kernel(
    sizes, l_hbm, theta_hbm, weight_ref, out_ref,
    lv, raw, th, wbuf, own, sbuf, rbuf, facc, yrecv, frecv, nrecv,
    l_sem, w_send, w_recv, raw_send, raw_recv, th_send, th_recv, c_send, c_recv,
    x_send, x_recv, fy_send, fy_recv, f_send, f_recv, n_send, n_recv, seen,
):
    n_chol, vectors, occupied, block_rows = sizes
    n_hi = n_chol // 2
    half = occupied // 2
    chunk_rows = 2 * block_rows
    theta_rows = 2 * block_rows
    n_groups = n_hi // 2
    last = n_hi - 1
    w = lax.axis_index("walker")
    s = lax.axis_index("slab")
    me = lax.axis_index("chol")
    z, y = me // 2, me % 2
    zn = z + 1 - 2 * (z % 2)
    sibling = {"walker": 1 - w}
    peer = {"slab": 1 - s}

    def chol(at, col):
        return {"chol": at * 2 + col}

    def partner(t):
        k = n_hi - 1 - t
        return lax.rem(z // 2 + k // 2, n_groups) * 2 + lax.rem(z + k, 2)

    def line(at):
        return jnp.logical_and(at >= 0, at < n_hi)

    def signal(sem, to):
        pl.semaphore_signal(sem, inc=1, device_id=to, device_id_type=MESH)

    def rdma(src, dst, send, recv, to):
        return pltpu.make_async_remote_copy(
            src_ref=src, dst_ref=dst, send_sem=send, recv_sem=recv, device_id=to, device_id_type=MESH
        )

    barrier = pltpu.get_barrier_semaphore()
    signal(barrier, sibling)
    signal(barrier, peer)
    signal(barrier, chol(z, 1 - y))
    for way in (-1, 1):

        @pl.when(line(z + way))
        def _():
            signal(barrier, chol(z + way, y))

    mine = pl.ds(pl.multiple_of(w * half, half), half)
    other = pl.ds(pl.multiple_of((1 - w) * half, half), half)
    keep = pltpu.make_async_copy(theta_hbm.at[0], raw.at[w], l_sem.at[2])
    load_mine = pltpu.make_async_copy(l_hbm.at[:, mine], lv.at[:, mine], l_sem.at[0])
    load_other = pltpu.make_async_copy(l_hbm.at[:, other], lv.at[:, other], l_sem.at[1])
    keep.start()
    load_mine.start()
    load_other.start()
    wbuf[w] = jnp.full(wbuf.shape[1:], weight_ref[0], jnp.float32)
    keep.wait()
    near = line(z - 1).astype(jnp.int32) + line(z + 1).astype(jnp.int32)
    pl.semaphore_wait(barrier, 3 + near)

    def give(walker):
        return rdma(raw.at[walker], raw.at[walker], raw_send, raw_recv, sibling)

    def give_weight(walker):
        return rdma(wbuf.at[walker], wbuf.at[walker], w_send, w_recv, sibling)

    give(w).start()
    give_weight(w).start()

    def vouch(stage, along_line):
        signal(seen.at[stage, 2], chol(z, 1 - y))
        if along_line:
            for d, way in enumerate((-1, 1)):

                @pl.when(line(z + way))
                def _():
                    signal(seen.at[stage, 1 - d], chol(z + way, y))

    def vouched(stage, along_line):
        pl.semaphore_wait(seen.at[stage, 2], 1)
        if along_line:
            for d, way in enumerate((-1, 1)):

                @pl.when(line(z + way))
                def _():
                    pl.semaphore_wait(seen.at[stage, d], 1)

    def spread(at, col):
        to = at * 2 + col
        return rdma(th.at[me, w], th.at[me, w], th_send.at[to], th_recv.at[me], {"chol": to})

    def spread_line(d, col):
        if d < n_hi:
            for way in (-1, 1):

                @pl.when(line(z + way * d))
                def _():
                    spread(z + way * d, col).start()

    vouch(0, True)
    give(1 - w).wait_recv()
    give_weight(1 - w).wait_recv()
    combined = wbuf[0][:1, :1] * raw[0].astype(jnp.float32) + wbuf[1][:1, :1] * raw[1].astype(jnp.float32)
    th[me] = combined.astype(jnp.bfloat16).reshape(th.shape[1:])
    spread(z, 1 - y).start()
    spread_line(1, y)

    def kind_of(kind):
        if kind == 0:
            return 4, 0, me, 1
        if kind == 1:
            return 4, 1, z * 2 + 1 - y, 1
        if kind == 2:
            return 2, 2, zn * 2, 2
        q = lax.rem(z // 2 + kind - 2, n_groups)
        return 1, 4 * (kind - 2), q * 4, 4

    unit = vectors // 4 * block_rows
    n_kinds = 3 + n_groups - 1

    def place(t, kind, h):
        pack, at, _, _ = kind_of(kind)
        span = pl.ds(at * unit, vectors // pack * block_rows)
        return (t, span) if h is None else (t, h, span)

    def xcopy(t, kind, h):
        if h is None:
            pick = (t, slice(None), place(t, kind, None)[1])
            sem = (t, kind, 0)
        else:
            pick = place(t, kind, h)
            sem = (t, kind, h)
        return rdma(sbuf.at[pick], rbuf.at[pick], x_send.at[sem], x_recv.at[sem], peer)

    def margins(t, kind, zt, h=None):
        pack, _, block, blocks = kind_of(kind)
        halves = (0, 1) if h is None else (h,)
        pieces = []
        for k in halves:
            start = w * half + zt * chunk_rows + k * block_rows
            rows = pl.ds(pl.multiple_of(start, block_rows), block_rows)
            pieces.append(lv[:, rows, :].reshape(vectors * block_rows, -1))
        x = pieces[0] if len(pieces) == 1 else jnp.concatenate(pieces, axis=0)
        theta = th[pl.ds(block, blocks)].reshape(blocks * theta_rows, -1)
        a = lax.dot_general(x, theta, NT, preferred_element_type=jnp.float32)
        per = vectors // pack * block_rows
        for i, k in enumerate(halves):
            parts = [a[(i * pack + p) * per : (i * pack + p + 1) * per] for p in range(pack)]
            packed = parts[0] if pack == 1 else jnp.concatenate(parts, axis=1)
            own[place(t, kind, k)] = packed
            sbuf[place(t, kind, k)] = packed.astype(jnp.bfloat16)
        xcopy(t, kind, h).start()

    def zt_of(t):
        return z if t == last else partner(t)

    load_mine.wait()

    def own_margins(t, carry):
        margins(t, 0, jnp.where(t == last, z, partner(t)))
        return carry

    step = max(1, n_hi // 2)
    lax.fori_loop(0, step, own_margins, 0)
    for stage in range(1, n_hi):
        vouched(stage - 1, stage < n_hi - 1)
        if stage < n_hi - 1:
            vouch(stage, stage < n_hi - 2)
        spread_line(stage + 1, y)
        spread_line(stage, 1 - y)
        if step < n_hi:
            own_margins(step, 0)
            step += 1

    def landed(block):
        rdma(th.at[block, w], th.at[block, w], c_send.at[0], th_recv.at[block], sibling).wait_recv()

    def hand(block):
        return rdma(th.at[block, w], th.at[block, w], c_send.at[block], c_recv.at[block], sibling)

    def relay(block):
        landed(block)
        hand(block).start()

    def handed(block):
        rdma(th.at[block, 1 - w], th.at[block, 1 - w], c_send.at[0], c_recv.at[block], sibling).wait_recv()

    y_block = z * 2 + 1 - y
    relay(y_block)
    relay(zn * 2 + y)
    handed(y_block)

    def y_margins(t, carry):
        margins(t, 1, partner(t))
        return carry

    lax.fori_loop(0, last, y_margins, 0)
    relay(zn * 2 + 1 - y)
    handed(zn * 2 + y)
    handed(zn * 2 + 1 - y)

    def z_margins(t, carry):
        margins(t, 2, partner(t))
        return carry

    lax.fori_loop(0, last - 1, z_margins, 0)
    for kind in range(3, n_kinds):
        q = lax.rem(z // 2 + kind - 2, n_groups)
        for col in (y, 1 - y):
            for k in range(2):
                relay(q * 4 + k * 2 + col)
    for kind in range(3, n_kinds):
        q = lax.rem(z // 2 + kind - 2, n_groups)
        for k in range(4):
            handed(q * 4 + k)

    def far_margins(t, carry):
        for kind in range(3, n_kinds):
            margins(t, kind, partner(t))
        return carry

    lax.fori_loop(0, last - 1, far_margins, 0)
    margins(last - 1, 2, partner(last - 1))
    far_margins(last - 1, 0)

    def small_margins(i, carry):
        h = jnp.where(i == 0, 1 - y, y)
        for kind in range(1, n_kinds):
            margins(last, kind, z, h)
        return carry

    lax.fori_loop(0, 2, small_margins, 0)
    load_other.wait()

    def fock(t, kinds, h=None):
        halves = (0, 1) if h is None else (h,)
        for kind in kinds:
            split = h is not None and kind > 0
            if h is None or split:
                xcopy(t, kind, h).wait_recv()
        lhs = []
        rhs = []
        for kind in kinds:
            pack, _, block, blocks = kind_of(kind)
            count = vectors // pack
            columns = []
            for k in halves:
                at = place(t, kind, k)
                total = own[at] + rbuf[at].astype(jnp.float32)
                columns.append(
                    jnp.concatenate([total[g * block_rows : (g + 1) * block_rows] for g in range(count)], axis=1)
                )
            lhs.append(columns[0] if len(columns) == 1 else jnp.concatenate(columns, axis=0))
            width = blocks * theta_rows
            m = pl.ds(pl.multiple_of(block * theta_rows, theta_rows), width)
            for g in range(count):
                for p in range(pack):
                    rhs.append(lv[p * count + g, m, :])
        total = lhs[0] if len(lhs) == 1 else jnp.concatenate(lhs, axis=1)
        high = total.astype(jnp.bfloat16)
        low = (total - high.astype(jnp.float32)).astype(jnp.bfloat16)
        both = jnp.dot(
            jnp.concatenate([high, low], axis=0),
            jnp.concatenate(rhs, axis=0),
            preferred_element_type=jnp.float32,
        )
        n = len(halves) * block_rows
        return both[:n] + both[n:]

    near_kinds = (0, 1, 2)
    far_kinds = tuple(range(3, n_kinds))

    def near_fock(t, carry):
        f = fock(t, near_kinds)
        for k in range(2):
            facc[t, k] = f[k * block_rows : (k + 1) * block_rows]
        return carry

    def far_fock(t):
        f = fock(t, far_kinds)
        for k in range(2):
            facc[t, k] = facc[t, k] + f[k * block_rows : (k + 1) * block_rows]

    def to_y(t):
        return rdma(facc.at[t, 1 - y], yrecv.at[t], fy_send.at[t], fy_recv.at[t], chol(z, 1 - y))

    def along_z(t):
        return rdma(facc.at[t, y], frecv.at[z], f_send.at[t], f_recv.at[z], chol(partner(t), y))

    def to_next(col):
        return rdma(facc.at[last - 1, col], nrecv.at[y], n_send.at[col], n_recv.at[y], chol(zn, col))

    def add_and_pass(t):
        to_y(t).wait_recv()
        facc[t, y] = facc[t, y] + yrecv[t]
        along_z(t).start()

    lax.fori_loop(0, last - 1, near_fock, 0)

    def far_step(t, carry):
        far_fock(t)
        to_y(t).start()
        return carry

    lax.fori_loop(0, last - 1, far_step, 0)
    near_fock(last - 1, 0)
    far_fock(last - 1)
    to_next(1 - y).start()
    to_next(y).start()
    for t in range(last - 2):
        add_and_pass(t)

    xcopy(last, 0, None).wait_recv()

    def small_fock(i, carry):
        h = jnp.where(i == 0, 1 - y, y)
        facc[last, h] = fock(last, near_kinds, h)
        facc[last, h] = facc[last, h] + fock(last, far_kinds, h)

        @pl.when(i == 0)
        def _():
            to_y(last).start()
            for t in range(max(0, last - 2), last - 1):
                add_and_pass(t)

        return carry

    lax.fori_loop(0, 2, small_fock, 0)

    result = facc[last, y]
    for t in range(last - 1):
        k = n_hi - 1 - t
        source = lax.rem(z // 2 + n_groups - k // 2, n_groups) * 2 + lax.rem(z + k, 2)
        rdma(frecv.at[source], frecv.at[source], f_send.at[0], f_recv.at[source], sibling).wait_recv()
        result = result + frecv[source]
    to_y(last).wait_recv()
    result = result + yrecv[last]
    for col in range(2):
        rdma(nrecv.at[col], nrecv.at[col], n_send.at[0], n_recv.at[col], sibling).wait_recv()
        result = result + nrecv[col]
    out_ref[...] = result

    give(w).wait_send()
    give_weight(w).wait_send()

    def drain_theta(to, carry):
        @pl.when(to != me)
        def _():
            spread(to // 2, to % 2).wait_send()
            hand(to).wait_send()

        return carry

    lax.fori_loop(0, n_chol, drain_theta, 0)

    def drain(t, carry):
        for kind in range(n_kinds):
            xcopy(t, kind, None).wait_send()
        return carry

    lax.fori_loop(0, last, drain, 0)
    xcopy(last, 0, None).wait_send()
    for kind in range(1, n_kinds):
        for h in range(2):
            xcopy(last, kind, h).wait_send()
    for t in range(last - 1):
        to_y(t).wait_send()
        along_z(t).wait_send()
    to_y(last).wait_send()
    for col in range(2):
        to_next(col).wait_send()


def fused(n_chol, cholesky_factors, greens, walker_weights):
    vectors, occupied, orbitals = cholesky_factors.shape
    block_rows = occupied // (2 * n_chol)
    n_hi = n_chol // 2
    n_groups = n_hi // 2
    width = 8 * block_rows
    rows = n_groups * vectors * block_rows
    n_kinds = n_groups + 2
    dma = pltpu.SemaphoreType.DMA
    return pl.pallas_call(
        functools.partial(exchange_kernel, (n_chol, vectors, occupied, block_rows)),
        out_shape=jax.ShapeDtypeStruct((block_rows, orbitals), jnp.float32),
        in_specs=[
            pl.BlockSpec(memory_space=pltpu.HBM),
            pl.BlockSpec(memory_space=pltpu.HBM),
            pl.BlockSpec(memory_space=pltpu.SMEM),
        ],
        out_specs=pl.BlockSpec(memory_space=pltpu.VMEM),
        scratch_shapes=[
            pltpu.VMEM((vectors, occupied, orbitals), jnp.bfloat16),
            pltpu.VMEM((2, 2 * block_rows, orbitals), jnp.bfloat16),
            pltpu.VMEM((n_chol, 2, block_rows, orbitals), jnp.bfloat16),
            pltpu.VMEM((2, 8, 128), jnp.float32),
            pltpu.VMEM((n_hi, 2, rows, width), jnp.float32),
            pltpu.VMEM((n_hi, 2, rows, width), jnp.bfloat16),
            pltpu.VMEM((n_hi, 2, rows, width), jnp.bfloat16),
            pltpu.VMEM((n_hi, 2, block_rows, orbitals), jnp.float32),
            pltpu.VMEM((n_hi, block_rows, orbitals), jnp.float32),
            pltpu.VMEM((n_hi, block_rows, orbitals), jnp.float32),
            pltpu.VMEM((2, block_rows, orbitals), jnp.float32),
            dma((3,)),
            dma,
            dma,
            dma,
            dma,
            dma((n_chol,)),
            dma((n_chol,)),
            dma((n_chol,)),
            dma((n_chol,)),
            dma((n_hi, n_kinds, 2)),
            dma((n_hi, n_kinds, 2)),
            dma((n_hi,)),
            dma((n_hi,)),
            dma((n_hi,)),
            dma((n_hi,)),
            dma((2,)),
            dma((2,)),
            pltpu.SemaphoreType.REGULAR((n_hi, 3)),
        ],
        compiler_params=pltpu.CompilerParams(
            collective_id=0, has_side_effects=True, vmem_limit_bytes=VMEM_LIMIT
        ),
    )(cholesky_factors, greens, walker_weights)


def plain(cholesky_factors, greens, walker_weights):
    panel_sum_terms = jnp.einsum(
        "gnp,mp->gnm",
        cholesky_factors,
        lax.all_gather(greens[0], "chol", axis=0, tiled=True),
        preferred_element_type=jnp.float32,
    )
    margin = lax.psum(panel_sum_terms, "slab").astype(jnp.bfloat16)
    terms = jnp.einsum("gnm,gmp->np", margin, cholesky_factors, preferred_element_type=jnp.float32)
    weighted = walker_weights[0] * terms
    return lax.psum_scatter(weighted, ("walker", "chol"), scatter_dimension=0, tiled=True)


def solution(mesh):
    walkers, slabs, n_chol = (mesh.shape[axis] for axis in ("walker", "slab", "chol"))

    def per_device(cholesky_factors, greens, walker_weights):
        vectors, occupied, _ = cholesky_factors.shape
        pair = walkers == 2 and slabs == 2 and greens.shape[0] == 1
        rows = occupied // n_chol
        fits = n_chol % 4 == 0 and n_chol >= 8 and vectors % 4 == 0 and occupied % (32 * n_chol) == 0 and 4 * rows == 128
        if pair and fits:
            return fused(n_chol, cholesky_factors, greens, walker_weights)
        return plain(cholesky_factors, greens, walker_weights)

    in_specs = (P("chol", None, "slab"), P("walker", "chol", "slab"), P("walker"))
    out_specs = P(("walker", "chol"), "slab")
    return jax.shard_map(
        per_device, mesh=mesh, in_specs=in_specs, out_specs=out_specs, check_vma=False
    )
```

```python
import functools

import jax
import jax.numpy as jnp
from jax import lax
from jax.experimental import pallas as pl
from jax.experimental.pallas import tpu as pltpu
from jax.sharding import PartitionSpec as P

MESH = pl.DeviceIdType.MESH
NT = (((1,), (1,)), ((), ()))
VMEM_LIMIT = 56000000


def exchange_kernel(
    sizes, l_hbm, theta_hbm, weight_ref, out_ref,
    lv, raw, th, wbuf, own, sbuf, rbuf, facc, yrecv, frecv, nrecv,
    l_sem, w_send, w_recv, raw_send, raw_recv, th_send, th_recv, c_send, c_recv,
    x_send, x_recv, fy_send, fy_recv, f_send, f_recv, n_send, n_recv, seen,
):
    n_chol, vectors, occupied, block_rows = sizes
    n_hi = n_chol // 2
    half = occupied // 2
    chunk_rows = 2 * block_rows
    theta_rows = 2 * block_rows
    n_groups = n_hi // 2
    last = n_hi - 1
    w = lax.axis_index("walker")
    s = lax.axis_index("slab")
    me = lax.axis_index("chol")
    z, y = me // 2, me % 2
    zn = z + 1 - 2 * (z % 2)
    sibling = {"walker": 1 - w}
    peer = {"slab": 1 - s}

    def chol(at, col):
        return {"chol": at * 2 + col}

    def partner(t):
        k = n_hi - 1 - t
        return lax.rem(z // 2 + k // 2, n_groups) * 2 + lax.rem(z + k, 2)

    def line(at):
        return jnp.logical_and(at >= 0, at < n_hi)

    def signal(sem, to):
        pl.semaphore_signal(sem, inc=1, device_id=to, device_id_type=MESH)

    def rdma(src, dst, send, recv, to):
        return pltpu.make_async_remote_copy(
            src_ref=src, dst_ref=dst, send_sem=send, recv_sem=recv, device_id=to, device_id_type=MESH
        )

    barrier = pltpu.get_barrier_semaphore()
    signal(barrier, sibling)
    signal(barrier, peer)
    signal(barrier, chol(z, 1 - y))
    for way in (-1, 1):

        @pl.when(line(z + way))
        def _():
            signal(barrier, chol(z + way, y))

    mine = pl.ds(pl.multiple_of(w * half, half), half)
    other = pl.ds(pl.multiple_of((1 - w) * half, half), half)
    keep = pltpu.make_async_copy(theta_hbm.at[0], raw.at[w], l_sem.at[2])
    load_mine = pltpu.make_async_copy(l_hbm.at[:, mine], lv.at[:, mine], l_sem.at[0])
    load_other = pltpu.make_async_copy(l_hbm.at[:, other], lv.at[:, other], l_sem.at[1])
    keep.start()
    load_mine.start()
    load_other.start()
    wbuf[w] = jnp.full(wbuf.shape[1:], weight_ref[0], jnp.float32)
    keep.wait()
    near = line(z - 1).astype(jnp.int32) + line(z + 1).astype(jnp.int32)
    pl.semaphore_wait(barrier, 3 + near)

    def give(walker):
        return rdma(raw.at[walker], raw.at[walker], raw_send, raw_recv, sibling)

    def give_weight(walker):
        return rdma(wbuf.at[walker], wbuf.at[walker], w_send, w_recv, sibling)

    give(w).start()
    give_weight(w).start()

    def vouch(stage, along_line):
        signal(seen.at[stage, 2], chol(z, 1 - y))
        if along_line:
            for d, way in enumerate((-1, 1)):

                @pl.when(line(z + way))
                def _():
                    signal(seen.at[stage, 1 - d], chol(z + way, y))

    def vouched(stage, along_line):
        pl.semaphore_wait(seen.at[stage, 2], 1)
        if along_line:
            for d, way in enumerate((-1, 1)):

                @pl.when(line(z + way))
                def _():
                    pl.semaphore_wait(seen.at[stage, d], 1)

    def spread(at, col):
        to = at * 2 + col
        return rdma(th.at[me, w], th.at[me, w], th_send.at[to], th_recv.at[me], {"chol": to})

    def spread_line(d, col):
        if d < n_hi:
            for way in (-1, 1):

                @pl.when(line(z + way * d))
                def _():
                    spread(z + way * d, col).start()

    vouch(0, True)
    give(1 - w).wait_recv()
    give_weight(1 - w).wait_recv()
    combined = wbuf[0][:1, :1] * raw[0].astype(jnp.float32) + wbuf[1][:1, :1] * raw[1].astype(jnp.float32)
    th[me] = combined.astype(jnp.bfloat16).reshape(th.shape[1:])
    spread(z, 1 - y).start()
    spread_line(1, y)

    def kind_of(kind):
        if kind == 0:
            return 4, 0, me, 1
        if kind == 1:
            return 4, 1, z * 2 + 1 - y, 1
        if kind == 2:
            return 2, 2, zn * 2, 2
        q = lax.rem(z // 2 + kind - 2, n_groups)
        return 1, 4 * (kind - 2), q * 4, 4

    unit = vectors // 4 * block_rows
    n_kinds = 3 + n_groups - 1

    def place(t, kind, h):
        pack, at, _, _ = kind_of(kind)
        span = pl.ds(at * unit, vectors // pack * block_rows)
        return (t, span) if h is None else (t, h, span)

    def xcopy(t, kind, h):
        if h is None:
            pick = (t, slice(None), place(t, kind, None)[1])
            sem = (t, kind, 0)
        else:
            pick = place(t, kind, h)
            sem = (t, kind, h)
        return rdma(sbuf.at[pick], rbuf.at[pick], x_send.at[sem], x_recv.at[sem], peer)

    def margins(t, kind, zt, h=None):
        pack, _, block, blocks = kind_of(kind)
        halves = (0, 1) if h is None else (h,)
        pieces = []
        for k in halves:
            start = w * half + zt * chunk_rows + k * block_rows
            rows = pl.ds(pl.multiple_of(start, block_rows), block_rows)
            pieces.append(lv[:, rows, :].reshape(vectors * block_rows, -1))
        x = pieces[0] if len(pieces) == 1 else jnp.concatenate(pieces, axis=0)
        theta = th[pl.ds(block, blocks)].reshape(blocks * theta_rows, -1)
        a = lax.dot_general(x, theta, NT, preferred_element_type=jnp.float32)
        per = vectors // pack * block_rows
        for i, k in enumerate(halves):
            parts = [a[(i * pack + p) * per : (i * pack + p + 1) * per] for p in range(pack)]
            packed = parts[0] if pack == 1 else jnp.concatenate(parts, axis=1)
            own[place(t, kind, k)] = packed
            sbuf[place(t, kind, k)] = packed.astype(jnp.bfloat16)
        xcopy(t, kind, h).start()

    def zt_of(t):
        return z if t == last else partner(t)

    def line_margins(kind):
        def body(t, carry):
            margins(t, kind, jnp.where(t == last, z, partner(t)))
            return carry

        return body

    for stage in range(1, n_hi):
        vouched(stage - 1, stage < n_hi - 1)
        if stage < n_hi - 1:
            vouch(stage, stage < n_hi - 2)
        spread_line(stage + 1, y)
        spread_line(stage, 1 - y)
        if stage == 1:
            load_mine.wait()
        line_margins(0)(stage - 1, 0)
    lax.fori_loop(last, n_hi, line_margins(0), 0)

    def landed(block):
        rdma(th.at[block, w], th.at[block, w], c_send.at[0], th_recv.at[block], sibling).wait_recv()

    def hand(block):
        return rdma(th.at[block, w], th.at[block, w], c_send.at[block], c_recv.at[block], sibling)

    def relay(block):
        landed(block)
        hand(block).start()

    def handed(block):
        rdma(th.at[block, 1 - w], th.at[block, 1 - w], c_send.at[0], c_recv.at[block], sibling).wait_recv()

    y_block = z * 2 + 1 - y
    relay(y_block)
    relay(zn * 2 + y)
    handed(y_block)

    lax.fori_loop(0, n_hi, line_margins(1), 0)
    relay(zn * 2 + 1 - y)
    handed(zn * 2 + y)
    handed(zn * 2 + 1 - y)

    def z_margins(t, carry):
        margins(t, 2, partner(t))
        return carry

    lax.fori_loop(0, last - 1, z_margins, 0)
    for kind in range(3, n_kinds):
        q = lax.rem(z // 2 + kind - 2, n_groups)
        for col in (y, 1 - y):
            for k in range(2):
                relay(q * 4 + k * 2 + col)
    for kind in range(3, n_kinds):
        q = lax.rem(z // 2 + kind - 2, n_groups)
        for k in range(4):
            handed(q * 4 + k)

    def far_margins(t, carry):
        for kind in range(3, n_kinds):
            margins(t, kind, partner(t))
        return carry

    lax.fori_loop(0, last - 1, far_margins, 0)
    margins(last - 1, 2, partner(last - 1))
    far_margins(last - 1, 0)

    def small_margins(i, carry):
        h = jnp.where(i == 0, 1 - y, y)
        for kind in range(2, n_kinds):
            margins(last, kind, z, h)
        return carry

    lax.fori_loop(0, 2, small_margins, 0)
    load_other.wait()

    def fock(t, kinds, h=None):
        halves = (0, 1) if h is None else (h,)
        for kind in kinds:
            split = h is not None and kind > 1
            if h is None or split:
                xcopy(t, kind, h).wait_recv()
        lhs = []
        rhs = []
        for kind in kinds:
            pack, _, block, blocks = kind_of(kind)
            count = vectors // pack
            columns = []
            for k in halves:
                at = place(t, kind, k)
                total = own[at] + rbuf[at].astype(jnp.float32)
                columns.append(
                    jnp.concatenate([total[g * block_rows : (g + 1) * block_rows] for g in range(count)], axis=1)
                )
            lhs.append(columns[0] if len(columns) == 1 else jnp.concatenate(columns, axis=0))
            width = blocks * theta_rows
            m = pl.ds(pl.multiple_of(block * theta_rows, theta_rows), width)
            for g in range(count):
                for p in range(pack):
                    rhs.append(lv[p * count + g, m, :])
        total = lhs[0] if len(lhs) == 1 else jnp.concatenate(lhs, axis=1)
        high = total.astype(jnp.bfloat16)
        low = (total - high.astype(jnp.float32)).astype(jnp.bfloat16)
        both = jnp.dot(
            jnp.concatenate([high, low], axis=0),
            jnp.concatenate(rhs, axis=0),
            preferred_element_type=jnp.float32,
        )
        n = len(halves) * block_rows
        return both[:n] + both[n:]

    near_kinds = (0, 1, 2)
    far_kinds = tuple(range(3, n_kinds))

    def near_fock(t, carry):
        f = fock(t, near_kinds)
        for k in range(2):
            facc[t, k] = f[k * block_rows : (k + 1) * block_rows]
        return carry

    def far_fock(t):
        f = fock(t, far_kinds)
        for k in range(2):
            facc[t, k] = facc[t, k] + f[k * block_rows : (k + 1) * block_rows]

    def to_y(t):
        return rdma(facc.at[t, 1 - y], yrecv.at[t], fy_send.at[t], fy_recv.at[t], chol(z, 1 - y))

    def along_z(t):
        return rdma(facc.at[t, y], frecv.at[z], f_send.at[t], f_recv.at[z], chol(partner(t), y))

    def direct(i, col):
        t = (0, last - 1)[i]
        to = chol(partner(t), col)
        return rdma(facc.at[t, col], nrecv.at[i, y], n_send.at[i, col], n_recv.at[i, y], to)

    def add_and_pass(t):
        to_y(t).wait_recv()
        facc[t, y] = facc[t, y] + yrecv[t]
        along_z(t).start()

    lax.fori_loop(0, last - 1, near_fock, 0)

    far_fock(0)
    direct(0, 1 - y).start()
    direct(0, y).start()

    def far_step(t, carry):
        far_fock(t)
        to_y(t).start()
        return carry

    lax.fori_loop(1, last - 1, far_step, 0)
    near_fock(last - 1, 0)
    far_fock(last - 1)
    direct(1, 1 - y).start()
    direct(1, y).start()
    for t in range(1, last - 1):
        add_and_pass(t)

    for kind in range(2):
        xcopy(last, kind, None).wait_recv()

    def small_fock(i, carry):
        h = jnp.where(i == 0, 1 - y, y)
        facc[last, h] = fock(last, near_kinds, h)
        facc[last, h] = facc[last, h] + fock(last, far_kinds, h)

        @pl.when(i == 0)
        def _():
            to_y(last).start()

        return carry

    lax.fori_loop(0, 2, small_fock, 0)

    result = facc[last, y]

    def take_direct(i):
        total = 0.0
        for col in range(2):
            rdma(nrecv.at[i, col], nrecv.at[i, col], n_send.at[0, 0], n_recv.at[i, col], sibling).wait_recv()
            total = total + nrecv[i, col]
        return total

    result = result + take_direct(0)
    for t in range(1, last - 1):
        k = n_hi - 1 - t
        source = lax.rem(z // 2 + n_groups - k // 2, n_groups) * 2 + lax.rem(z + k, 2)
        rdma(frecv.at[source], frecv.at[source], f_send.at[0], f_recv.at[source], sibling).wait_recv()
        result = result + frecv[source]
    to_y(last).wait_recv()
    result = result + yrecv[last]
    result = result + take_direct(1)
    out_ref[...] = result

    give(w).wait_send()
    give_weight(w).wait_send()

    def drain_theta(to, carry):
        @pl.when(to != me)
        def _():
            spread(to // 2, to % 2).wait_send()
            hand(to).wait_send()

        return carry

    lax.fori_loop(0, n_chol, drain_theta, 0)

    def drain(t, carry):
        for kind in range(n_kinds):
            xcopy(t, kind, None).wait_send()
        return carry

    lax.fori_loop(0, last, drain, 0)
    for kind in range(2):
        xcopy(last, kind, None).wait_send()
    for kind in range(2, n_kinds):
        for h in range(2):
            xcopy(last, kind, h).wait_send()
    for t in range(1, last - 1):
        to_y(t).wait_send()
        along_z(t).wait_send()
    to_y(last).wait_send()
    for i in range(2):
        for col in range(2):
            direct(i, col).wait_send()


def fused(n_chol, cholesky_factors, greens, walker_weights):
    vectors, occupied, orbitals = cholesky_factors.shape
    block_rows = occupied // (2 * n_chol)
    n_hi = n_chol // 2
    n_groups = n_hi // 2
    width = 8 * block_rows
    rows = n_groups * vectors * block_rows
    n_kinds = n_groups + 2
    dma = pltpu.SemaphoreType.DMA
    return pl.pallas_call(
        functools.partial(exchange_kernel, (n_chol, vectors, occupied, block_rows)),
        out_shape=jax.ShapeDtypeStruct((block_rows, orbitals), jnp.float32),
        in_specs=[
            pl.BlockSpec(memory_space=pltpu.HBM),
            pl.BlockSpec(memory_space=pltpu.HBM),
            pl.BlockSpec(memory_space=pltpu.SMEM),
        ],
        out_specs=pl.BlockSpec(memory_space=pltpu.VMEM),
        scratch_shapes=[
            pltpu.VMEM((vectors, occupied, orbitals), jnp.bfloat16),
            pltpu.VMEM((2, 2 * block_rows, orbitals), jnp.bfloat16),
            pltpu.VMEM((n_chol, 2, block_rows, orbitals), jnp.bfloat16),
            pltpu.VMEM((2, 8, 128), jnp.float32),
            pltpu.VMEM((n_hi, 2, rows, width), jnp.float32),
            pltpu.VMEM((n_hi, 2, rows, width), jnp.bfloat16),
            pltpu.VMEM((n_hi, 2, rows, width), jnp.bfloat16),
            pltpu.VMEM((n_hi, 2, block_rows, orbitals), jnp.float32),
            pltpu.VMEM((n_hi, block_rows, orbitals), jnp.float32),
            pltpu.VMEM((n_hi, block_rows, orbitals), jnp.float32),
            pltpu.VMEM((2, 2, block_rows, orbitals), jnp.float32),
            dma((3,)),
            dma,
            dma,
            dma,
            dma,
            dma((n_chol,)),
            dma((n_chol,)),
            dma((n_chol,)),
            dma((n_chol,)),
            dma((n_hi, n_kinds, 2)),
            dma((n_hi, n_kinds, 2)),
            dma((n_hi,)),
            dma((n_hi,)),
            dma((n_hi,)),
            dma((n_hi,)),
            dma((2, 2)),
            dma((2, 2)),
            pltpu.SemaphoreType.REGULAR((n_hi, 3)),
        ],
        compiler_params=pltpu.CompilerParams(
            collective_id=0, has_side_effects=True, vmem_limit_bytes=VMEM_LIMIT
        ),
    )(cholesky_factors, greens, walker_weights)


def plain(cholesky_factors, greens, walker_weights):
    panel_sum_terms = jnp.einsum(
        "gnp,mp->gnm",
        cholesky_factors,
        lax.all_gather(greens[0], "chol", axis=0, tiled=True),
        preferred_element_type=jnp.float32,
    )
    margin = lax.psum(panel_sum_terms, "slab").astype(jnp.bfloat16)
    terms = jnp.einsum("gnm,gmp->np", margin, cholesky_factors, preferred_element_type=jnp.float32)
    weighted = walker_weights[0] * terms
    return lax.psum_scatter(weighted, ("walker", "chol"), scatter_dimension=0, tiled=True)


def solution(mesh):
    walkers, slabs, n_chol = (mesh.shape[axis] for axis in ("walker", "slab", "chol"))

    def per_device(cholesky_factors, greens, walker_weights):
        vectors, occupied, _ = cholesky_factors.shape
        pair = walkers == 2 and slabs == 2 and greens.shape[0] == 1
        rows = occupied // n_chol
        fits = n_chol % 4 == 0 and n_chol >= 8 and vectors % 4 == 0 and occupied % (32 * n_chol) == 0 and 4 * rows == 128
        if pair and fits:
            return fused(n_chol, cholesky_factors, greens, walker_weights)
        return plain(cholesky_factors, greens, walker_weights)

    in_specs = (P("chol", None, "slab"), P("walker", "chol", "slab"), P("walker"))
    out_specs = P(("walker", "chol"), "slab")
    return jax.shard_map(
        per_device, mesh=mesh, in_specs=in_specs, out_specs=out_specs, check_vma=False
    )
```

```python
import functools

import jax
import jax.numpy as jnp
from jax import lax
from jax.experimental import pallas as pl
from jax.experimental.pallas import tpu as pltpu
from jax.sharding import PartitionSpec as P

MESH = pl.DeviceIdType.MESH
NT = (((1,), (1,)), ((), ()))


def exchange_kernel(
    sizes, l_hbm, theta_hbm, weight_ref, out_ref,
    lv, raw, th, rest, wbuf, own, sbuf, rbuf, facc, yrecv, nrecv, bsend, brecv,
    l_sem, w_send, w_recv, raw_send, raw_recv, rest_send, rest_recv, th_send, th_recv, c_send, c_recv,
    x_send, x_recv, fy_send, fy_recv, f_send, f_recv, n_send, n_recv, seen,
):
    n_chol, vectors, occupied, block_rows = sizes
    n_hi = n_chol // 2
    half = occupied // 2
    chunk_rows = 2 * block_rows
    theta_rows = 2 * block_rows
    n_groups = n_hi // 2
    last = n_hi - 1
    w = lax.axis_index("walker")
    s = lax.axis_index("slab")
    me = lax.axis_index("chol")
    z, y = me // 2, me % 2
    zn = z + 1 - 2 * (z % 2)
    sibling = {"walker": 1 - w}
    peer = {"slab": 1 - s}

    def chol(at, col):
        return {"chol": at * 2 + col}

    def partner(t):
        k = n_hi - 1 - t
        return lax.rem(z // 2 + k // 2, n_groups) * 2 + lax.rem(z + k, 2)

    def line(at):
        return jnp.logical_and(at >= 0, at < n_hi)

    def signal(sem, to):
        pl.semaphore_signal(sem, inc=1, device_id=to, device_id_type=MESH)

    def rdma(src, dst, send, recv, to):
        return pltpu.make_async_remote_copy(
            src_ref=src, dst_ref=dst, send_sem=send, recv_sem=recv, device_id=to, device_id_type=MESH
        )

    barrier = pltpu.get_barrier_semaphore()
    leads = w == 0
    signal(barrier, {"slab": 1 - s, "walker": 0})

    @pl.when(leads)
    def _():
        signal(barrier, sibling)
        signal(barrier, chol(z, 1 - y))
        for way in (-1, 1):

            @pl.when(line(z + way))
            def _():
                signal(barrier, chol(z + way, y))

    mine = pl.ds(pl.multiple_of(w * half, half), half)
    other = pl.ds(pl.multiple_of((1 - w) * half, half), half)
    load_mine = pltpu.make_async_copy(l_hbm.at[:, mine], lv.at[:, mine], l_sem.at[0])
    load_other = pltpu.make_async_copy(l_hbm.at[:, other], lv.at[:, other], l_sem.at[1])
    keep = pltpu.make_async_copy(theta_hbm.at[0], raw.at[0], l_sem.at[2])
    give = rdma(theta_hbm.at[0], raw.at[1], raw_send, raw_recv, sibling)
    give_weight = rdma(wbuf.at[1], wbuf.at[1], w_send, w_recv, sibling)

    def vouch(stage, along_line):
        signal(seen.at[stage, 2], chol(z, 1 - y))
        if along_line:
            for d, way in enumerate((-1, 1)):

                @pl.when(line(z + way))
                def _():
                    signal(seen.at[stage, 1 - d], chol(z + way, y))

    def vouched(stage, along_line):
        pl.semaphore_wait(seen.at[stage, 2], 1)
        if along_line:
            for d, way in enumerate((-1, 1)):

                @pl.when(line(z + way))
                def _():
                    pl.semaphore_wait(seen.at[stage, d], 1)

    def spread(at, col):
        to = at * 2 + col
        return rdma(th.at[me], th.at[me], th_send.at[to], th_recv.at[me], {"chol": to})

    def spread_line(d, col):
        if d < n_hi:
            for way in (-1, 1):

                @pl.when(line(z + way * d))
                def _():
                    spread(z + way * d, col).start()

    def hand(block):
        return rdma(th.at[block], th.at[block], c_send.at[block], c_recv.at[block], sibling)

    hand_rest = rdma(rest, rest, rest_send, rest_recv, sibling)

    def relay(block):
        rdma(th.at[block], th.at[block], c_send.at[block], th_recv.at[block], sibling).wait_recv()
        hand(block).start()

    def gather(*blocks):
        @pl.when(leads)
        def _():
            for block in blocks:
                relay(block)

        @pl.when(jnp.logical_not(leads))
        def _():
            for block in blocks:
                hand(block).wait_recv()

    wbuf[w] = jnp.full(wbuf.shape[1:], weight_ref[0], jnp.float32)

    @pl.when(jnp.logical_not(leads))
    def _():
        pl.semaphore_wait(barrier, 1)
        give.start()
        give_weight.start()
        load_mine.start()
        load_other.start()
        hand(me).wait_recv()
        hand_rest.wait_recv()

    @pl.when(leads)
    def _():
        keep.start()
        load_mine.start()
        load_other.start()
        keep.wait()
        give.wait_recv()
        give_weight.wait_recv()
        combined = wbuf[0][:1, :1] * raw[0].astype(jnp.float32) + wbuf[1][:1, :1] * raw[1].astype(jnp.float32)
        rounded = combined.astype(jnp.bfloat16)
        th[me] = rounded
        rest[...] = (combined - rounded.astype(jnp.float32)).astype(jnp.bfloat16)
        near = line(z - 1).astype(jnp.int32) + line(z + 1).astype(jnp.int32)
        pl.semaphore_wait(barrier, 3 + near)
        vouch(0, True)
        spread(z, 1 - y).start()
        spread_line(1, y)
        hand(me).start()
        hand_rest.start()

    def kind_of(kind):
        if kind == 0:
            return 4, 0, me, 1
        if kind == 1:
            return 4, 1, z * 2 + 1 - y, 1
        if kind == 2:
            return 2, 2, zn * 2, 2
        q = lax.rem(z // 2 + kind - 2, n_groups)
        return 1, 4 * (kind - 2), q * 4, 4

    unit = vectors // 4 * block_rows
    n_kinds = 3 + n_groups - 1

    def place(t, kind, h):
        pack, at, _, _ = kind_of(kind)
        span = pl.ds(at * unit, vectors // pack * block_rows)
        return (t, span) if h is None else (t, h, span)

    def xcopy(t, kind, h):
        if h is None:
            pick = (t, slice(None), place(t, kind, None)[1])
            sem = (t, kind, 0)
        else:
            pick = place(t, kind, h)
            sem = (t, kind, h)
        return rdma(sbuf.at[pick], rbuf.at[pick], x_send.at[sem], x_recv.at[sem], peer)

    def margins(t, kind, zt, h=None):
        pack, _, block, blocks = kind_of(kind)
        halves = (0, 1) if h is None else (h,)
        pieces = []
        for k in halves:
            start = w * half + zt * chunk_rows + k * block_rows
            rows = pl.ds(pl.multiple_of(start, block_rows), block_rows)
            pieces.append(lv[:, rows, :].reshape(vectors * block_rows, -1))
        x = pieces[0] if len(pieces) == 1 else jnp.concatenate(pieces, axis=0)
        theta = th[pl.ds(block, blocks)].reshape(blocks * theta_rows, -1)
        if kind == 0:
            theta = jnp.concatenate([theta, rest[...]], axis=0)
        a = lax.dot_general(x, theta, NT, preferred_element_type=jnp.float32)
        if kind == 0:
            a = a[:, :theta_rows] + a[:, theta_rows:]
        per = vectors // pack * block_rows
        for i, k in enumerate(halves):
            parts = [a[(i * pack + p) * per : (i * pack + p + 1) * per] for p in range(pack)]
            packed = parts[0] if pack == 1 else jnp.concatenate(parts, axis=1)
            own[place(t, kind, k)] = packed
            sbuf[place(t, kind, k)] = packed.astype(jnp.bfloat16)
        xcopy(t, kind, h).start()

    def zt_of(t):
        return z if t == last else partner(t)

    def line_margins(kind):
        def body(t, carry):
            margins(t, kind, jnp.where(t == last, z, partner(t)))
            return carry

        return body

    def vouching(stage):
        vouched(stage - 1, stage < n_hi - 1)
        if stage < n_hi - 1:
            vouch(stage, stage < n_hi - 2)
        spread_line(stage + 1, y)
        spread_line(stage, 1 - y)

    load_mine.wait()
    line_margins(0)(0, 0)

    @pl.when(leads)
    def _():
        vouching(1)

    lax.fori_loop(1, n_hi, line_margins(0), 0)

    @pl.when(leads)
    def _():
        for stage in range(2, last):
            vouching(stage)

    gather(z * 2 + 1 - y)
    line_margins(1)(0, 0)

    @pl.when(leads)
    def _():
        vouching(last)

    lax.fori_loop(1, n_hi, line_margins(1), 0)
    gather(zn * 2 + y, zn * 2 + 1 - y)

    def z_margins(t, carry):
        margins(t, 2, partner(t))
        return carry

    lax.fori_loop(0, last, z_margins, 0)
    for kind in range(3, n_kinds):
        q = lax.rem(z // 2 + kind - 2, n_groups)
        gather(*(q * 4 + k * 2 + col for col in (y, 1 - y) for k in range(2)))

    def far_margins(t, carry):
        for kind in range(3, n_kinds):
            margins(t, kind, partner(t))
        return carry

    lax.fori_loop(0, last, far_margins, 0)

    def small_margins(i, carry):
        h = jnp.where(i == 0, 1 - y, y)
        for kind in range(2, n_kinds):
            margins(last, kind, z, h)
        return carry

    lax.fori_loop(0, 2, small_margins, 0)
    load_other.wait()

    def fock(t, kinds, h=None):
        halves = (0, 1) if h is None else (h,)
        for kind in kinds:
            split = h is not None and kind > 1
            if h is None or split:
                xcopy(t, kind, h).wait_recv()
        lhs = []
        rhs = []
        for kind in kinds:
            pack, _, block, blocks = kind_of(kind)
            count = vectors // pack
            columns = []
            for k in halves:
                at = place(t, kind, k)
                total = own[at] + rbuf[at].astype(jnp.float32)
                columns.append(
                    jnp.concatenate([total[g * block_rows : (g + 1) * block_rows] for g in range(count)], axis=1)
                )
            lhs.append(columns[0] if len(columns) == 1 else jnp.concatenate(columns, axis=0))
            width = blocks * theta_rows
            m = pl.ds(pl.multiple_of(block * theta_rows, theta_rows), width)
            for g in range(count):
                for p in range(pack):
                    rhs.append(lv[p * count + g, m, :])
        total = lhs[0] if len(lhs) == 1 else jnp.concatenate(lhs, axis=1)
        high = total.astype(jnp.bfloat16)
        low = (total - high.astype(jnp.float32)).astype(jnp.bfloat16)
        both = jnp.dot(
            jnp.concatenate([high, low], axis=0),
            jnp.concatenate(rhs, axis=0),
            preferred_element_type=jnp.float32,
        )
        n = len(halves) * block_rows
        return both[:n] + both[n:]

    near_kinds = (0, 1, 2)
    far_kinds = tuple(range(3, n_kinds))

    def near_fock(t, carry):
        f = fock(t, near_kinds)
        for k in range(2):
            facc[t, k] = f[k * block_rows : (k + 1) * block_rows]
        return carry

    def far_fock(t):
        f = fock(t, far_kinds)
        for k in range(2):
            facc[t, k] = facc[t, k] + f[k * block_rows : (k + 1) * block_rows]

    def to_y():
        return rdma(facc.at[last, 1 - y], yrecv, fy_send, fy_recv, chol(z, 1 - y))

    def cross(t, col):
        return rdma(bsend.at[t, col], brecv.at[t, y], f_send.at[t, col], f_recv.at[t, y], chol(partner(t), col))

    def direct(col):
        return rdma(facc.at[last - 1, col], nrecv.at[y], n_send.at[col], n_recv.at[y], chol(zn, col))

    lax.fori_loop(0, last, near_fock, 0)

    def far_step(t, carry):
        far_fock(t)
        bsend[t] = facc[t].astype(jnp.bfloat16)
        cross(t, 1 - y).start()
        cross(t, y).start()
        return carry

    lax.fori_loop(0, last - 1, far_step, 0)
    far_fock(last - 1)
    direct(1 - y).start()
    direct(y).start()

    for kind in range(2):
        xcopy(last, kind, None).wait_recv()

    def small_fock(i, carry):
        h = jnp.where(i == 0, 1 - y, y)
        facc[last, h] = fock(last, near_kinds, h)
        facc[last, h] = facc[last, h] + fock(last, far_kinds, h)

        @pl.when(i == 0)
        def _():
            to_y().start()

        return carry

    lax.fori_loop(0, 2, small_fock, 0)

    result = facc[last, y]

    for t in range(last - 1):
        for col in range(2):
            rdma(brecv.at[t, col], brecv.at[t, col], f_send.at[0, 0], f_recv.at[t, col], sibling).wait_recv()
            result = result + brecv[t, col].astype(jnp.float32)
    to_y().wait_recv()
    result = result + yrecv[...]
    for col in range(2):
        rdma(nrecv.at[col], nrecv.at[col], n_send.at[0], n_recv.at[col], sibling).wait_recv()
        result = result + nrecv[col]
    out_ref[...] = result

    @pl.when(jnp.logical_not(leads))
    def _():
        give.wait_send()
        give_weight.wait_send()

    @pl.when(leads)
    def _():
        def drain_theta(to, carry):
            hand(to).wait_send()

            @pl.when(to != me)
            def _():
                spread(to // 2, to % 2).wait_send()

            return carry

        lax.fori_loop(0, n_chol, drain_theta, 0)
        hand_rest.wait_send()

    def drain(t, carry):
        for kind in range(n_kinds):
            xcopy(t, kind, None).wait_send()
        return carry

    lax.fori_loop(0, last, drain, 0)
    for kind in range(2):
        xcopy(last, kind, None).wait_send()
    for kind in range(2, n_kinds):
        for h in range(2):
            xcopy(last, kind, h).wait_send()
    to_y().wait_send()
    for col in range(2):
        for t in range(last - 1):
            cross(t, col).wait_send()
        direct(col).wait_send()


def fused(n_chol, cholesky_factors, greens, walker_weights):
    vectors, occupied, orbitals = cholesky_factors.shape
    block_rows = occupied // (2 * n_chol)
    n_hi = n_chol // 2
    n_groups = n_hi // 2
    width = 8 * block_rows
    rows = n_groups * vectors * block_rows
    n_kinds = n_groups + 2
    dma = pltpu.SemaphoreType.DMA
    return pl.pallas_call(
        functools.partial(exchange_kernel, (n_chol, vectors, occupied, block_rows)),
        out_shape=pltpu.VMEM((block_rows, orbitals), jnp.float32),
        in_specs=[
            pl.BlockSpec(memory_space=pltpu.HBM),
            pl.BlockSpec(memory_space=pltpu.HBM),
            pl.BlockSpec(memory_space=pltpu.SMEM),
        ],
        out_specs=pl.BlockSpec(memory_space=pltpu.VMEM),
        scratch_shapes=[
            pltpu.VMEM((vectors, occupied, orbitals), jnp.bfloat16),
            pltpu.VMEM((2, 2 * block_rows, orbitals), jnp.bfloat16),
            pltpu.VMEM((n_chol, 2 * block_rows, orbitals), jnp.bfloat16),
            pltpu.VMEM((2 * block_rows, orbitals), jnp.bfloat16),
            pltpu.VMEM((2, 8, 128), jnp.float32),
            pltpu.VMEM((n_hi, 2, rows, width), jnp.float32),
            pltpu.VMEM((n_hi, 2, rows, width), jnp.bfloat16),
            pltpu.VMEM((n_hi, 2, rows, width), jnp.bfloat16),
            pltpu.VMEM((n_hi, 2, block_rows, orbitals), jnp.float32),
            pltpu.VMEM((block_rows, orbitals), jnp.float32),
            pltpu.VMEM((2, block_rows, orbitals), jnp.float32),
            pltpu.VMEM((n_hi - 2, 2, block_rows, orbitals), jnp.bfloat16),
            pltpu.VMEM((n_hi - 2, 2, block_rows, orbitals), jnp.bfloat16),
            dma((3,)),
            dma,
            dma,
            dma,
            dma,
            dma,
            dma,
            dma((n_chol,)),
            dma((n_chol,)),
            dma((n_chol,)),
            dma((n_chol,)),
            dma((n_hi, n_kinds, 2)),
            dma((n_hi, n_kinds, 2)),
            dma,
            dma,
            dma((n_hi - 2, 2)),
            dma((n_hi - 2, 2)),
            dma((2,)),
            dma((2,)),
            pltpu.SemaphoreType.REGULAR((n_hi, 3)),
        ],
        compiler_params=pltpu.CompilerParams(
            collective_id=0, has_side_effects=True
        ),
    )(cholesky_factors, greens, walker_weights)


def plain(cholesky_factors, greens, walker_weights):
    panel_sum_terms = jnp.einsum(
        "gnp,mp->gnm",
        cholesky_factors,
        lax.all_gather(greens[0], "chol", axis=0, tiled=True),
        preferred_element_type=jnp.float32,
    )
    margin = lax.psum(panel_sum_terms, "slab").astype(jnp.bfloat16)
    terms = jnp.einsum("gnm,gmp->np", margin, cholesky_factors, preferred_element_type=jnp.float32)
    weighted = walker_weights[0] * terms
    return lax.psum_scatter(weighted, ("walker", "chol"), scatter_dimension=0, tiled=True)


def solution(mesh):
    walkers, slabs, n_chol = (mesh.shape[axis] for axis in ("walker", "slab", "chol"))

    def per_device(cholesky_factors, greens, walker_weights):
        vectors, occupied, _ = cholesky_factors.shape
        pair = walkers == 2 and slabs == 2 and greens.shape[0] == 1
        rows = occupied // n_chol
        fits = n_chol % 4 == 0 and n_chol >= 8 and vectors % 4 == 0 and occupied % (32 * n_chol) == 0 and 4 * rows == 128
        if pair and fits:
            return fused(n_chol, cholesky_factors, greens, walker_weights)
        return plain(cholesky_factors, greens, walker_weights)

    in_specs = (P("chol", None, "slab"), P("walker", "chol", "slab"), P("walker"))
    out_specs = P(("walker", "chol"), "slab")
    return jax.shard_map(
        per_device, mesh=mesh, in_specs=in_specs, out_specs=out_specs, check_vma=False
    )
```

```python
import functools

import jax
import jax.numpy as jnp
from jax import lax
from jax.experimental import pallas as pl
from jax.experimental.pallas import tpu as pltpu
from jax.sharding import PartitionSpec as P

MESH = pl.DeviceIdType.MESH
NT = (((1,), (1,)), ((), ()))


def exchange_kernel(
    sizes, l_hbm, theta_hbm, weight_ref, out_ref,
    lv, raw, th, rest, wbuf, own, sbuf, rbuf, facc, yrecv, nrecv, bsend, brecv,
    l_sem, w_send, w_recv, raw_send, raw_recv, rest_send, rest_recv, th_send, th_recv, c_send, c_recv,
    x_send, x_recv, fy_send, fy_recv, f_send, f_recv, n_send, n_recv, seen,
):
    n_chol, vectors, occupied, block_rows = sizes
    n_hi = n_chol // 2
    half = occupied // 2
    chunk_rows = 2 * block_rows
    theta_rows = 2 * block_rows
    n_groups = n_hi // 2
    last = n_hi - 1
    w = lax.axis_index("walker")
    s = lax.axis_index("slab")
    me = lax.axis_index("chol")
    z, y = me // 2, me % 2
    zn = z + 1 - 2 * (z % 2)
    sibling = {"walker": 1 - w}
    peer = {"slab": 1 - s}

    def chol(at, col):
        return {"chol": at * 2 + col}

    def partner(t):
        k = n_hi - 1 - t
        return lax.rem(z // 2 + k // 2, n_groups) * 2 + lax.rem(z + k, 2)

    def line(at):
        return jnp.logical_and(at >= 0, at < n_hi)

    def signal(sem, to):
        pl.semaphore_signal(sem, inc=1, device_id=to, device_id_type=MESH)

    def rdma(src, dst, send, recv, to):
        return pltpu.make_async_remote_copy(
            src_ref=src, dst_ref=dst, send_sem=send, recv_sem=recv, device_id=to, device_id_type=MESH
        )

    barrier = pltpu.get_barrier_semaphore()
    leads = w == 0
    signal(barrier, {"slab": 1 - s, "walker": 0})

    @pl.when(leads)
    def _():
        signal(barrier, sibling)
        signal(barrier, chol(z, 1 - y))
        for way in (-1, 1):

            @pl.when(line(z + way))
            def _():
                signal(barrier, chol(z + way, y))

    mine = pl.ds(pl.multiple_of(w * half, half), half)
    other = pl.ds(pl.multiple_of((1 - w) * half, half), half)
    load_mine = pltpu.make_async_copy(l_hbm.at[:, mine], lv.at[:, mine], l_sem.at[0])
    load_other = pltpu.make_async_copy(l_hbm.at[:, other], lv.at[:, other], l_sem.at[1])
    keep = pltpu.make_async_copy(theta_hbm.at[0], raw.at[0], l_sem.at[2])
    give = rdma(theta_hbm.at[0], raw.at[1], raw_send, raw_recv, sibling)
    give_weight = rdma(wbuf.at[1], wbuf.at[1], w_send, w_recv, sibling)

    def vouch(stage, along_line):
        signal(seen.at[stage, 2], chol(z, 1 - y))
        if along_line:
            for d, way in enumerate((-1, 1)):

                @pl.when(line(z + way))
                def _():
                    signal(seen.at[stage, 1 - d], chol(z + way, y))

    def vouched(stage, along_line):
        pl.semaphore_wait(seen.at[stage, 2], 1)
        if along_line:
            for d, way in enumerate((-1, 1)):

                @pl.when(line(z + way))
                def _():
                    pl.semaphore_wait(seen.at[stage, d], 1)

    def spread(at, col):
        to = at * 2 + col
        return rdma(th.at[me], th.at[me], th_send.at[to], th_recv.at[me], {"chol": to})

    def spread_line(d, col):
        if d < n_hi:
            for way in (-1, 1):

                @pl.when(line(z + way * d))
                def _():
                    spread(z + way * d, col).start()

    def hand(block):
        return rdma(th.at[block], th.at[block], c_send.at[block], c_recv.at[block], sibling)

    hand_rest = rdma(rest, rest, rest_send, rest_recv, sibling)

    def relay(block):
        rdma(th.at[block], th.at[block], c_send.at[block], th_recv.at[block], sibling).wait_recv()
        hand(block).start()

    def gather(*blocks):
        @pl.when(leads)
        def _():
            for block in blocks:
                relay(block)

        @pl.when(jnp.logical_not(leads))
        def _():
            for block in blocks:
                hand(block).wait_recv()

    wbuf[w] = jnp.full(wbuf.shape[1:], weight_ref[0], jnp.float32)

    @pl.when(jnp.logical_not(leads))
    def _():
        pl.semaphore_wait(barrier, 1)
        give.start()
        give_weight.start()
        load_mine.start()
        load_other.start()
        hand(me).wait_recv()
        hand_rest.wait_recv()

    @pl.when(leads)
    def _():
        keep.start()
        load_mine.start()
        load_other.start()
        keep.wait()
        give.wait_recv()
        give_weight.wait_recv()
        combined = wbuf[0][:1, :1] * raw[0].astype(jnp.float32) + wbuf[1][:1, :1] * raw[1].astype(jnp.float32)
        rounded = combined.astype(jnp.bfloat16)
        th[me] = rounded
        rest[...] = (combined - rounded.astype(jnp.float32)).astype(jnp.bfloat16)
        near = line(z - 1).astype(jnp.int32) + line(z + 1).astype(jnp.int32)
        pl.semaphore_wait(barrier, 3 + near)
        vouch(0, True)
        spread(z, 1 - y).start()
        spread_line(1, y)
        hand(me).start()
        hand_rest.start()

    def kind_of(kind):
        if kind == 0:
            return 4, 0, me, 1
        if kind == 1:
            return 4, 1, z * 2 + 1 - y, 1
        if kind == 2:
            return 2, 2, zn * 2, 2
        q = lax.rem(z // 2 + kind - 2, n_groups)
        return 1, 4 * (kind - 2), q * 4, 4

    unit = vectors // 4 * block_rows
    n_kinds = 3 + n_groups - 1

    def place(t, kind, h):
        pack, at, _, _ = kind_of(kind)
        span = pl.ds(at * unit, vectors // pack * block_rows)
        return (t, span) if h is None else (t, h, span)

    def xcopy(t, kind, h):
        if h is None:
            pick = (t, slice(None), place(t, kind, None)[1])
            sem = (t, kind, 0)
        else:
            pick = place(t, kind, h)
            sem = (t, kind, h)
        return rdma(sbuf.at[pick], rbuf.at[pick], x_send.at[sem], x_recv.at[sem], peer)

    def margins(t, kind, zt, h=None):
        pack, _, block, blocks = kind_of(kind)
        halves = (0, 1) if h is None else (h,)
        pieces = []
        for k in halves:
            start = w * half + zt * chunk_rows + k * block_rows
            rows = pl.ds(pl.multiple_of(start, block_rows), block_rows)
            pieces.append(lv[:, rows, :].reshape(vectors * block_rows, -1))
        x = pieces[0] if len(pieces) == 1 else jnp.concatenate(pieces, axis=0)
        theta = th[pl.ds(block, blocks)].reshape(blocks * theta_rows, -1)
        if kind == 0:
            theta = jnp.concatenate([theta, rest[...]], axis=0)
        a = lax.dot_general(x, theta, NT, preferred_element_type=jnp.float32)
        if kind == 0:
            a = a[:, :theta_rows] + a[:, theta_rows:]
        per = vectors // pack * block_rows
        for i, k in enumerate(halves):
            parts = [a[(i * pack + p) * per : (i * pack + p + 1) * per] for p in range(pack)]
            packed = parts[0] if pack == 1 else jnp.concatenate(parts, axis=1)
            own[place(t, kind, k)] = packed
            sbuf[place(t, kind, k)] = packed.astype(jnp.bfloat16)
        xcopy(t, kind, h).start()

    def zt_of(t):
        return z if t == last else partner(t)

    def line_margins(kind):
        def body(t, carry):
            margins(t, kind, jnp.where(t == last, z, partner(t)))
            return carry

        return body

    def vouching(stage):
        vouched(stage - 1, stage < n_hi - 1)
        if stage < n_hi - 1:
            vouch(stage, stage < n_hi - 2)
        spread_line(stage + 1, y)
        spread_line(stage, 1 - y)

    load_mine.wait()
    line_margins(0)(0, 0)

    @pl.when(leads)
    def _():
        vouching(1)

    lax.fori_loop(1, n_hi, line_margins(0), 0)

    @pl.when(leads)
    def _():
        for stage in range(2, last):
            vouching(stage)

    gather(z * 2 + 1 - y)
    line_margins(1)(0, 0)

    @pl.when(leads)
    def _():
        vouching(last)

    lax.fori_loop(1, n_hi, line_margins(1), 0)
    gather(zn * 2 + y, zn * 2 + 1 - y)

    def z_margins(t, carry):
        margins(t, 2, partner(t))
        return carry

    lax.fori_loop(0, last, z_margins, 0)
    for kind in range(3, n_kinds):
        q = lax.rem(z // 2 + kind - 2, n_groups)
        gather(*(q * 4 + k * 2 + col for col in (y, 1 - y) for k in range(2)))

    def far_margins(t, carry):
        for kind in range(3, n_kinds):
            margins(t, kind, partner(t))
        return carry

    def far_turn(i, carry):
        return far_margins(jnp.where(i == 0, 0, last - i), carry)

    lax.fori_loop(0, last, far_turn, 0)

    def small_margins(i, carry):
        h = jnp.where(i == 0, 1 - y, y)
        for kind in range(2, n_kinds):
            margins(last, kind, z, h)
        return carry

    lax.fori_loop(0, 2, small_margins, 0)
    load_other.wait()

    def fock(t, kinds, h=None):
        halves = (0, 1) if h is None else (h,)
        for kind in kinds:
            split = h is not None and kind > 1
            if h is None or split:
                xcopy(t, kind, h).wait_recv()
        lhs = []
        rhs = []
        for kind in kinds:
            pack, _, block, blocks = kind_of(kind)
            count = vectors // pack
            columns = []
            for k in halves:
                at = place(t, kind, k)
                total = own[at] + rbuf[at].astype(jnp.float32)
                columns.append(
                    jnp.concatenate([total[g * block_rows : (g + 1) * block_rows] for g in range(count)], axis=1)
                )
            lhs.append(columns[0] if len(columns) == 1 else jnp.concatenate(columns, axis=0))
            width = blocks * theta_rows
            m = pl.ds(pl.multiple_of(block * theta_rows, theta_rows), width)
            for g in range(count):
                for p in range(pack):
                    rhs.append(lv[p * count + g, m, :])
        total = lhs[0] if len(lhs) == 1 else jnp.concatenate(lhs, axis=1)
        high = total.astype(jnp.bfloat16)
        low = (total - high.astype(jnp.float32)).astype(jnp.bfloat16)
        both = jnp.dot(
            jnp.concatenate([high, low], axis=0),
            jnp.concatenate(rhs, axis=0),
            preferred_element_type=jnp.float32,
        )
        n = len(halves) * block_rows
        return both[:n] + both[n:]

    near_kinds = (0, 1, 2)
    far_kinds = tuple(range(3, n_kinds))

    def near_fock(t, carry):
        f = fock(t, near_kinds)
        for k in range(2):
            facc[t, k] = f[k * block_rows : (k + 1) * block_rows]
        return carry

    def far_fock(t):
        f = fock(t, far_kinds)
        for k in range(2):
            facc[t, k] = facc[t, k] + f[k * block_rows : (k + 1) * block_rows]

    def to_y():
        return rdma(facc.at[last, 1 - y], yrecv, fy_send, fy_recv, chol(z, 1 - y))

    def cross(t, col):
        return rdma(bsend.at[t, col], brecv.at[t, y], f_send.at[t, col], f_recv.at[t, y], chol(partner(t), col))

    def direct(col):
        return rdma(facc.at[last - 1, col], nrecv.at[y], n_send.at[col], n_recv.at[y], chol(zn, col))

    lax.fori_loop(0, last, near_fock, 0)

    def far_step(t, carry):
        far_fock(t)
        bsend[t] = facc[t].astype(jnp.bfloat16)
        cross(t, 1 - y).start()
        cross(t, y).start()
        return carry

    far_step(0, 0)
    far_fock(last - 1)
    direct(1 - y).start()
    direct(y).start()
    lax.fori_loop(1, last - 1, far_step, 0)

    for kind in range(2):
        xcopy(last, kind, None).wait_recv()

    def small_fock(i, carry):
        h = jnp.where(i == 0, 1 - y, y)
        facc[last, h] = fock(last, near_kinds, h)
        facc[last, h] = facc[last, h] + fock(last, far_kinds, h)

        @pl.when(i == 0)
        def _():
            to_y().start()

        return carry

    lax.fori_loop(0, 2, small_fock, 0)

    result = facc[last, y]

    for t in range(last - 1):
        for col in range(2):
            rdma(brecv.at[t, col], brecv.at[t, col], f_send.at[0, 0], f_recv.at[t, col], sibling).wait_recv()
            result = result + brecv[t, col].astype(jnp.float32)
    to_y().wait_recv()
    result = result + yrecv[...]
    for col in range(2):
        rdma(nrecv.at[col], nrecv.at[col], n_send.at[0], n_recv.at[col], sibling).wait_recv()
        result = result + nrecv[col]
    out_ref[...] = result

    @pl.when(jnp.logical_not(leads))
    def _():
        give.wait_send()
        give_weight.wait_send()

    @pl.when(leads)
    def _():
        def drain_theta(to, carry):
            hand(to).wait_send()

            @pl.when(to != me)
            def _():
                spread(to // 2, to % 2).wait_send()

            return carry

        lax.fori_loop(0, n_chol, drain_theta, 0)
        hand_rest.wait_send()

    def drain(t, carry):
        for kind in range(n_kinds):
            xcopy(t, kind, None).wait_send()
        return carry

    lax.fori_loop(0, last, drain, 0)
    for kind in range(2):
        xcopy(last, kind, None).wait_send()
    for kind in range(2, n_kinds):
        for h in range(2):
            xcopy(last, kind, h).wait_send()
    to_y().wait_send()
    for col in range(2):
        for t in range(last - 1):
            cross(t, col).wait_send()
        direct(col).wait_send()


def fused(n_chol, cholesky_factors, greens, walker_weights):
    vectors, occupied, orbitals = cholesky_factors.shape
    block_rows = occupied // (2 * n_chol)
    n_hi = n_chol // 2
    n_groups = n_hi // 2
    width = 8 * block_rows
    rows = n_groups * vectors * block_rows
    n_kinds = n_groups + 2
    dma = pltpu.SemaphoreType.DMA
    return pl.pallas_call(
        functools.partial(exchange_kernel, (n_chol, vectors, occupied, block_rows)),
        out_shape=pltpu.VMEM((block_rows, orbitals), jnp.float32),
        in_specs=[
            pl.BlockSpec(memory_space=pltpu.HBM),
            pl.BlockSpec(memory_space=pltpu.HBM),
            pl.BlockSpec(memory_space=pltpu.SMEM),
        ],
        out_specs=pl.BlockSpec(memory_space=pltpu.VMEM),
        scratch_shapes=[
            pltpu.VMEM((vectors, occupied, orbitals), jnp.bfloat16),
            pltpu.VMEM((2, 2 * block_rows, orbitals), jnp.bfloat16),
            pltpu.VMEM((n_chol, 2 * block_rows, orbitals), jnp.bfloat16),
            pltpu.VMEM((2 * block_rows, orbitals), jnp.bfloat16),
            pltpu.VMEM((2, 8, 128), jnp.float32),
            pltpu.VMEM((n_hi, 2, rows, width), jnp.float32),
            pltpu.VMEM((n_hi, 2, rows, width), jnp.bfloat16),
            pltpu.VMEM((n_hi, 2, rows, width), jnp.bfloat16),
            pltpu.VMEM((n_hi, 2, block_rows, orbitals), jnp.float32),
            pltpu.VMEM((block_rows, orbitals), jnp.float32),
            pltpu.VMEM((2, block_rows, orbitals), jnp.float32),
            pltpu.VMEM((n_hi - 2, 2, block_rows, orbitals), jnp.bfloat16),
            pltpu.VMEM((n_hi - 2, 2, block_rows, orbitals), jnp.bfloat16),
            dma((3,)),
            dma,
            dma,
            dma,
            dma,
            dma,
            dma,
            dma((n_chol,)),
            dma((n_chol,)),
            dma((n_chol,)),
            dma((n_chol,)),
            dma((n_hi, n_kinds, 2)),
            dma((n_hi, n_kinds, 2)),
            dma,
            dma,
            dma((n_hi - 2, 2)),
            dma((n_hi - 2, 2)),
            dma((2,)),
            dma((2,)),
            pltpu.SemaphoreType.REGULAR((n_hi, 3)),
        ],
        compiler_params=pltpu.CompilerParams(
            collective_id=0, has_side_effects=True
        ),
    )(cholesky_factors, greens, walker_weights)


def plain(cholesky_factors, greens, walker_weights):
    panel_sum_terms = jnp.einsum(
        "gnp,mp->gnm",
        cholesky_factors,
        lax.all_gather(greens[0], "chol", axis=0, tiled=True),
        preferred_element_type=jnp.float32,
    )
    margin = lax.psum(panel_sum_terms, "slab").astype(jnp.bfloat16)
    terms = jnp.einsum("gnm,gmp->np", margin, cholesky_factors, preferred_element_type=jnp.float32)
    weighted = walker_weights[0] * terms
    return lax.psum_scatter(weighted, ("walker", "chol"), scatter_dimension=0, tiled=True)


def solution(mesh):
    walkers, slabs, n_chol = (mesh.shape[axis] for axis in ("walker", "slab", "chol"))

    def per_device(cholesky_factors, greens, walker_weights):
        vectors, occupied, _ = cholesky_factors.shape
        pair = walkers == 2 and slabs == 2 and greens.shape[0] == 1
        rows = occupied // n_chol
        fits = n_chol % 4 == 0 and n_chol >= 8 and vectors % 4 == 0 and occupied % (32 * n_chol) == 0 and 4 * rows == 128
        if pair and fits:
            return fused(n_chol, cholesky_factors, greens, walker_weights)
        return plain(cholesky_factors, greens, walker_weights)

    in_specs = (P("chol", None, "slab"), P("walker", "chol", "slab"), P("walker"))
    out_specs = P(("walker", "chol"), "slab")
    return jax.shard_map(
        per_device, mesh=mesh, in_specs=in_specs, out_specs=out_specs, check_vma=False
    )
```

```python
import functools

import jax
import jax.numpy as jnp
from jax import lax
from jax.experimental import pallas as pl
from jax.experimental.pallas import tpu as pltpu
from jax.sharding import PartitionSpec as P

MESH = pl.DeviceIdType.MESH
NT = (((1,), (1,)), ((), ()))


def exchange_kernel(
    sizes, l_hbm, theta_hbm, weight_ref, out_ref,
    lv, raw, th, rest, wbuf, own, sbuf, rbuf, facc, yrecv, nrecv, bsend, brecv,
    l_sem, w_send, w_recv, raw_send, raw_recv, rest_send, rest_recv, th_send, th_recv, c_send, c_recv,
    x_send, x_recv, fy_send, fy_recv, f_send, f_recv, n_send, n_recv, seen,
):
    n_chol, vectors, occupied, block_rows = sizes
    n_hi = n_chol // 2
    half = occupied // 2
    chunk_rows = 2 * block_rows
    theta_rows = 2 * block_rows
    n_groups = n_hi // 2
    last = n_hi - 1
    w = lax.axis_index("walker")
    s = lax.axis_index("slab")
    me = lax.axis_index("chol")
    z, y = me // 2, me % 2
    zn = z + 1 - 2 * (z % 2)
    sibling = {"walker": 1 - w}
    peer = {"slab": 1 - s}

    def chol(at, col):
        return {"chol": at * 2 + col}

    def partner(t):
        k = n_hi - 1 - t
        return lax.rem(z // 2 + k // 2, n_groups) * 2 + lax.rem(z + k, 2)

    def line(at):
        return jnp.logical_and(at >= 0, at < n_hi)

    def signal(sem, to):
        pl.semaphore_signal(sem, inc=1, device_id=to, device_id_type=MESH)

    def rdma(src, dst, send, recv, to):
        return pltpu.make_async_remote_copy(
            src_ref=src, dst_ref=dst, send_sem=send, recv_sem=recv, device_id=to, device_id_type=MESH
        )

    barrier = pltpu.get_barrier_semaphore()
    leads = w == 0
    signal(barrier, {"slab": 1 - s, "walker": 0})

    @pl.when(leads)
    def _():
        signal(barrier, sibling)
        signal(barrier, chol(z, 1 - y))
        for way in (-1, 1):

            @pl.when(line(z + way))
            def _():
                signal(barrier, chol(z + way, y))

    mine = pl.ds(pl.multiple_of(w * half, half), half)
    other = pl.ds(pl.multiple_of((1 - w) * half, half), half)
    load_mine = pltpu.make_async_copy(l_hbm.at[:, mine], lv.at[:, mine], l_sem.at[0])
    load_other = pltpu.make_async_copy(l_hbm.at[:, other], lv.at[:, other], l_sem.at[1])
    keep = pltpu.make_async_copy(theta_hbm.at[0], raw.at[0], l_sem.at[2])
    give = rdma(theta_hbm.at[0], raw.at[1], raw_send, raw_recv, sibling)
    give_weight = rdma(wbuf.at[1], wbuf.at[1], w_send, w_recv, sibling)

    def vouch(stage, along_line):
        signal(seen.at[stage, 2], chol(z, 1 - y))
        if along_line:
            for d, way in enumerate((-1, 1)):

                @pl.when(line(z + way))
                def _():
                    signal(seen.at[stage, 1 - d], chol(z + way, y))

    def vouched(stage, along_line):
        pl.semaphore_wait(seen.at[stage, 2], 1)
        if along_line:
            for d, way in enumerate((-1, 1)):

                @pl.when(line(z + way))
                def _():
                    pl.semaphore_wait(seen.at[stage, d], 1)

    def spread(at, col):
        to = at * 2 + col
        return rdma(th.at[me], th.at[me], th_send.at[to], th_recv.at[me], {"chol": to})

    def spread_line(d, col):
        if d < n_hi:
            for way in (-1, 1):

                @pl.when(line(z + way * d))
                def _():
                    spread(z + way * d, col).start()

    def hand(block):
        return rdma(th.at[block], th.at[block], c_send.at[block], c_recv.at[block], sibling)

    hand_rest = rdma(rest, rest, rest_send, rest_recv, sibling)

    def relay(block):
        rdma(th.at[block], th.at[block], c_send.at[block], th_recv.at[block], sibling).wait_recv()
        hand(block).start()

    def gather(*blocks):
        @pl.when(leads)
        def _():
            for block in blocks:
                relay(block)

        @pl.when(jnp.logical_not(leads))
        def _():
            for block in blocks:
                hand(block).wait_recv()

    wbuf[w] = jnp.full(wbuf.shape[1:], weight_ref[0], jnp.float32)

    @pl.when(jnp.logical_not(leads))
    def _():
        pl.semaphore_wait(barrier, 1)
        give.start()
        give_weight.start()
        load_mine.start()
        load_other.start()
        hand(me).wait_recv()
        hand_rest.wait_recv()

    @pl.when(leads)
    def _():
        keep.start()
        load_mine.start()
        load_other.start()
        keep.wait()
        give.wait_recv()
        give_weight.wait_recv()
        combined = wbuf[0][:1, :1] * raw[0].astype(jnp.float32) + wbuf[1][:1, :1] * raw[1].astype(jnp.float32)
        rounded = combined.astype(jnp.bfloat16)
        th[me] = rounded
        rest[...] = (combined - rounded.astype(jnp.float32)).astype(jnp.bfloat16)
        near = line(z - 1).astype(jnp.int32) + line(z + 1).astype(jnp.int32)
        pl.semaphore_wait(barrier, 3 + near)
        spread(z, 1 - y).start()
        spread_line(1, y)
        vouch(0, True)
        hand(me).start()
        hand_rest.start()

    def kind_of(kind):
        if kind == 0:
            return 4, 0, me, 1
        if kind == 1:
            return 4, 1, z * 2 + 1 - y, 1
        if kind == 2:
            return 2, 2, zn * 2, 2
        q = lax.rem(z // 2 + kind - 2, n_groups)
        return 1, 4 * (kind - 2), q * 4, 4

    unit = vectors // 4 * block_rows
    n_kinds = 3 + n_groups - 1

    def place(t, kind, h):
        pack, at, _, _ = kind_of(kind)
        span = pl.ds(at * unit, vectors // pack * block_rows)
        return (t, span) if h is None else (t, h, span)

    def xcopy(t, kind, h):
        if h is None:
            pick = (t, slice(None), place(t, kind, None)[1])
            sem = (t, kind, 0)
        else:
            pick = place(t, kind, h)
            sem = (t, kind, h)
        return rdma(sbuf.at[pick], rbuf.at[pick], x_send.at[sem], x_recv.at[sem], peer)

    def margins(t, kind, zt, h=None):
        pack, _, block, blocks = kind_of(kind)
        halves = (0, 1) if h is None else (h,)
        pieces = []
        for k in halves:
            start = w * half + zt * chunk_rows + k * block_rows
            rows = pl.ds(pl.multiple_of(start, block_rows), block_rows)
            pieces.append(lv[:, rows, :].reshape(vectors * block_rows, -1))
        x = pieces[0] if len(pieces) == 1 else jnp.concatenate(pieces, axis=0)
        theta = th[pl.ds(block, blocks)].reshape(blocks * theta_rows, -1)
        if kind == 0:
            theta = jnp.concatenate([theta, rest[...]], axis=0)
        a = lax.dot_general(x, theta, NT, preferred_element_type=jnp.float32)
        if kind == 0:
            a = a[:, :theta_rows] + a[:, theta_rows:]
        per = vectors // pack * block_rows
        for i, k in enumerate(halves):
            parts = [a[(i * pack + p) * per : (i * pack + p + 1) * per] for p in range(pack)]
            packed = parts[0] if pack == 1 else jnp.concatenate(parts, axis=1)
            own[place(t, kind, k)] = packed
            sbuf[place(t, kind, k)] = packed.astype(jnp.bfloat16)
        xcopy(t, kind, h).start()

    def zt_of(t):
        return z if t == last else partner(t)

    def line_margins(kind):
        def body(t, carry):
            margins(t, kind, jnp.where(t == last, z, partner(t)))
            return carry

        return body

    def vouching(stage):
        vouched(stage - 1, stage < n_hi - 1)
        if stage < n_hi - 1:
            vouch(stage, stage < n_hi - 2)
        spread_line(stage + 1, y)
        spread_line(stage, 1 - y)

    load_mine.wait()
    line_margins(0)(0, 0)

    @pl.when(leads)
    def _():
        vouching(1)

    lax.fori_loop(1, n_hi, line_margins(0), 0)

    @pl.when(leads)
    def _():
        for stage in range(2, last):
            vouching(stage)

    early = zn * 2 + y

    @pl.when(leads)
    def _():
        relay(z * 2 + 1 - y)
        relay(early)

    @pl.when(jnp.logical_not(leads))
    def _():
        hand(z * 2 + 1 - y).wait_recv()

    line_margins(1)(0, 0)

    @pl.when(leads)
    def _():
        vouching(last)

    lax.fori_loop(1, n_hi, line_margins(1), 0)
    gather(zn * 2 + 1 - y)

    @pl.when(jnp.logical_not(leads))
    def _():
        hand(early).wait_recv()


    def z_margins(t, carry):
        margins(t, 2, partner(t))
        return carry

    lax.fori_loop(0, last, z_margins, 0)
    for kind in range(3, n_kinds):
        q = lax.rem(z // 2 + kind - 2, n_groups)
        gather(*(q * 4 + k * 2 + col for col in (y, 1 - y) for k in range(2)))

    def far_margins(t, carry):
        for kind in range(3, n_kinds):
            margins(t, kind, partner(t))
        return carry

    def far_turn(i, carry):
        return far_margins(jnp.where(i == 0, 0, last - i), carry)

    lax.fori_loop(0, last, far_turn, 0)

    def small_margins(i, carry):
        h = jnp.where(i == 0, 1 - y, y)
        for kind in range(2, n_kinds):
            margins(last, kind, z, h)
        return carry

    lax.fori_loop(0, 2, small_margins, 0)
    load_other.wait()

    span = lv.shape[2] // 2

    def fock(t, kinds, h=None, c=None):
        halves = (0, 1) if h is None else (h,)
        cols = slice(None) if c is None else slice(c * span, (c + 1) * span)
        for kind in kinds if c != 1 else ():
            split = h is not None and kind > 1
            if h is None or split:
                xcopy(t, kind, h).wait_recv()
        lhs = []
        rhs = []
        for kind in kinds:
            pack, _, block, blocks = kind_of(kind)
            count = vectors // pack
            columns = []
            for k in halves:
                at = place(t, kind, k)
                total = own[at] + rbuf[at].astype(jnp.float32)
                columns.append(
                    jnp.concatenate([total[g * block_rows : (g + 1) * block_rows] for g in range(count)], axis=1)
                )
            lhs.append(columns[0] if len(columns) == 1 else jnp.concatenate(columns, axis=0))
            width = blocks * theta_rows
            m = pl.ds(pl.multiple_of(block * theta_rows, theta_rows), width)
            for g in range(count):
                for p in range(pack):
                    rhs.append(lv[p * count + g, m, cols])
        total = lhs[0] if len(lhs) == 1 else jnp.concatenate(lhs, axis=1)
        high = total.astype(jnp.bfloat16)
        low = (total - high.astype(jnp.float32)).astype(jnp.bfloat16)
        both = jnp.dot(
            jnp.concatenate([high, low], axis=0),
            jnp.concatenate(rhs, axis=0),
            preferred_element_type=jnp.float32,
        )
        n = len(halves) * block_rows
        return both[:n] + both[n:]

    near_kinds = (0, 1, 2)
    far_kinds = tuple(range(3, n_kinds))

    def near_fock(t, carry):
        f = fock(t, near_kinds)
        for k in range(2):
            facc[t, k] = f[k * block_rows : (k + 1) * block_rows]
        return carry

    def far_fock(t):
        f = fock(t, far_kinds)
        for k in range(2):
            facc[t, k] = facc[t, k] + f[k * block_rows : (k + 1) * block_rows]

    def to_y(c):
        cols = slice(c * span, (c + 1) * span)
        return rdma(facc.at[last, 1 - y, :, cols], yrecv.at[:, cols], fy_send.at[c], fy_recv.at[c], chol(z, 1 - y))

    def cross(t, col):
        return rdma(bsend.at[t, col], brecv.at[t, y], f_send.at[t, col], f_recv.at[t, y], chol(partner(t), col))

    def direct(col):
        return rdma(facc.at[last - 1, col], nrecv.at[y], n_send.at[col], n_recv.at[y], chol(zn, col))

    lax.fori_loop(0, last, near_fock, 0)

    def far_step(t, carry):
        far_fock(t)
        bsend[t] = facc[t].astype(jnp.bfloat16)
        cross(t, 1 - y).start()
        cross(t, y).start()
        return carry

    far_step(0, 0)
    far_fock(last - 1)
    direct(1 - y).start()
    direct(y).start()
    lax.fori_loop(1, last - 1, far_step, 0)

    for kind in range(2):
        xcopy(last, kind, None).wait_recv()

    def small_fock(i, carry):
        h = jnp.where(i == 0, 1 - y, y)
        facc[last, h] = fock(last, near_kinds, h)
        for c in range(2):
            cols = slice(c * span, (c + 1) * span)
            facc[last, h, :, cols] = facc[last, h, :, cols] + fock(last, far_kinds, h, c)

            @pl.when(i == 0)
            def _():
                to_y(c).start()

        return carry

    lax.fori_loop(0, 2, small_fock, 0)

    result = facc[last, y]

    for t in range(last - 1):
        for col in range(2):
            rdma(brecv.at[t, col], brecv.at[t, col], f_send.at[0, 0], f_recv.at[t, col], sibling).wait_recv()
            result = result + brecv[t, col].astype(jnp.float32)
    for c in range(2):
        to_y(c).wait_recv()
    result = result + yrecv[...]
    for col in range(2):
        rdma(nrecv.at[col], nrecv.at[col], n_send.at[0], n_recv.at[col], sibling).wait_recv()
        result = result + nrecv[col]
    out_ref[...] = result

    @pl.when(jnp.logical_not(leads))
    def _():
        give.wait_send()
        give_weight.wait_send()

    @pl.when(leads)
    def _():
        def drain_theta(to, carry):
            hand(to).wait_send()

            @pl.when(to != me)
            def _():
                spread(to // 2, to % 2).wait_send()

            return carry

        lax.fori_loop(0, n_chol, drain_theta, 0)
        hand_rest.wait_send()

    def drain(t, carry):
        for kind in range(n_kinds):
            xcopy(t, kind, None).wait_send()
        return carry

    lax.fori_loop(0, last, drain, 0)
    for kind in range(2):
        xcopy(last, kind, None).wait_send()
    for kind in range(2, n_kinds):
        for h in range(2):
            xcopy(last, kind, h).wait_send()
    for c in range(2):
        to_y(c).wait_send()
    for col in range(2):
        for t in range(last - 1):
            cross(t, col).wait_send()
        direct(col).wait_send()


def fused(n_chol, cholesky_factors, greens, walker_weights):
    vectors, occupied, orbitals = cholesky_factors.shape
    block_rows = occupied // (2 * n_chol)
    n_hi = n_chol // 2
    n_groups = n_hi // 2
    width = 8 * block_rows
    rows = n_groups * vectors * block_rows
    n_kinds = n_groups + 2
    dma = pltpu.SemaphoreType.DMA
    return pl.pallas_call(
        functools.partial(exchange_kernel, (n_chol, vectors, occupied, block_rows)),
        out_shape=pltpu.VMEM((block_rows, orbitals), jnp.float32),
        in_specs=[
            pl.BlockSpec(memory_space=pltpu.HBM),
            pl.BlockSpec(memory_space=pltpu.HBM),
            pl.BlockSpec(memory_space=pltpu.SMEM),
        ],
        out_specs=pl.BlockSpec(memory_space=pltpu.VMEM),
        scratch_shapes=[
            pltpu.VMEM((vectors, occupied, orbitals), jnp.bfloat16),
            pltpu.VMEM((2, 2 * block_rows, orbitals), jnp.bfloat16),
            pltpu.VMEM((n_chol, 2 * block_rows, orbitals), jnp.bfloat16),
            pltpu.VMEM((2 * block_rows, orbitals), jnp.bfloat16),
            pltpu.VMEM((2, 8, 128), jnp.float32),
            pltpu.VMEM((n_hi, 2, rows, width), jnp.float32),
            pltpu.VMEM((n_hi, 2, rows, width), jnp.bfloat16),
            pltpu.VMEM((n_hi, 2, rows, width), jnp.bfloat16),
            pltpu.VMEM((n_hi, 2, block_rows, orbitals), jnp.float32),
            pltpu.VMEM((block_rows, orbitals), jnp.float32),
            pltpu.VMEM((2, block_rows, orbitals), jnp.float32),
            pltpu.VMEM((n_hi - 2, 2, block_rows, orbitals), jnp.bfloat16),
            pltpu.VMEM((n_hi - 2, 2, block_rows, orbitals), jnp.bfloat16),
            dma((3,)),
            dma,
            dma,
            dma,
            dma,
            dma,
            dma,
            dma((n_chol,)),
            dma((n_chol,)),
            dma((n_chol,)),
            dma((n_chol,)),
            dma((n_hi, n_kinds, 2)),
            dma((n_hi, n_kinds, 2)),
            dma((2,)),
            dma((2,)),
            dma((n_hi - 2, 2)),
            dma((n_hi - 2, 2)),
            dma((2,)),
            dma((2,)),
            pltpu.SemaphoreType.REGULAR((n_hi, 3)),
        ],
        compiler_params=pltpu.CompilerParams(
            collective_id=0, has_side_effects=True
        ),
    )(cholesky_factors, greens, walker_weights)


def plain(cholesky_factors, greens, walker_weights):
    panel_sum_terms = jnp.einsum(
        "gnp,mp->gnm",
        cholesky_factors,
        lax.all_gather(greens[0], "chol", axis=0, tiled=True),
        preferred_element_type=jnp.float32,
    )
    margin = lax.psum(panel_sum_terms, "slab").astype(jnp.bfloat16)
    terms = jnp.einsum("gnm,gmp->np", margin, cholesky_factors, preferred_element_type=jnp.float32)
    weighted = walker_weights[0] * terms
    return lax.psum_scatter(weighted, ("walker", "chol"), scatter_dimension=0, tiled=True)


def solution(mesh):
    walkers, slabs, n_chol = (mesh.shape[axis] for axis in ("walker", "slab", "chol"))

    def per_device(cholesky_factors, greens, walker_weights):
        vectors, occupied, _ = cholesky_factors.shape
        pair = walkers == 2 and slabs == 2 and greens.shape[0] == 1
        rows = occupied // n_chol
        fits = n_chol % 4 == 0 and n_chol >= 8 and vectors % 4 == 0 and occupied % (32 * n_chol) == 0 and 4 * rows == 128
        if pair and fits:
            return fused(n_chol, cholesky_factors, greens, walker_weights)
        return plain(cholesky_factors, greens, walker_weights)

    in_specs = (P("chol", None, "slab"), P("walker", "chol", "slab"), P("walker"))
    out_specs = P(("walker", "chol"), "slab")
    return jax.shard_map(
        per_device, mesh=mesh, in_specs=in_specs, out_specs=out_specs, check_vma=False
    )
```
